32 devices in a mesh: leaf: 8 (over z, x), panel: 4 (over y, core).
Axes of the slice: x: 2, y: 2, z: 4, core: 2. Of those that a mesh axis runs over, the one named last changes fastest.
Arguments:
- adjoint_rhs: float32 [8, 64, 3840], P('leaf', None, 'panel'), may hold values from -6 to 6
- panel_tiles: bfloat16 [8, 2048, 8704], P('leaf', 'panel'), may hold values from -0.0625 to 0.0625
- diag_inverse: bfloat16 [8, 3840, 2048], P('leaf', 'panel'), may hold values from -0.125 to 0.125
- front_sizes: int32 [15], replicated, may hold values from 512 to 2048
Outputs:
- solution: float32 [8, 4, 64, 2048], P('leaf', None, None, 'panel')
The draws below stay inside these ranges and needn't reach their ends.
All inputs are finite; a program needn't handle non-finite values.
Results may differ from the reference program's by a relative error of at most 0.0051.
Values sent between devices are 32-bit elements; how exact they have to be, the bound alone decides.
No kernel may reach another device: no remote copies, remote signals or barrier semaphores. Data moves between devices by JAX's collectives and lax.ppermute only.
A program may use at most 128 MiB of HBM per device.

```python
import jax
import jax.numpy as jnp
from jax import lax

SEP = 2048
NRHS = 64
LEVELS = 4
NODES = 15
PCOLS = 8704
DROWS = 3840
N_LEAF = 8
N_PANEL = 4


def plant(drawn, own_key, low, top_value):
    index_at = [jax.random.randint(jax.random.fold_in(own_key, axis), (), 0, length) for axis, length in enumerate(drawn.shape)]
    main_axis = drawn.shape.index(max(drawn.shape))
    neighbour = index_at[:main_axis] + [(index_at[main_axis] + 1) % drawn.shape[main_axis]] + index_at[main_axis + 1:]
    return drawn.at[tuple(index_at)].set(low).at[tuple(neighbour)].set(top_value)


def shard_levels(stream_key, shape, pieces, smallest, high):
    def one(axis_at, shards_of):
        heights = jax.random.uniform(jax.random.fold_in(jax.random.fold_in(stream_key, 6), axis_at), (shards_of,), jnp.float32, smallest / len(pieces), high / len(pieces))
        return jnp.repeat(jnp.exp(heights), shape[axis_at] // shards_of).reshape((-1,) + (1,) * (len(shape) - axis_at - 1))

    factor_of = one(*pieces[0])
    for cut in pieces[1:]:
        factor_of = factor_of * one(*cut)
    return factor_of


def centred(own_key, shape, deviation, limit, pieces=(), kind=jnp.bfloat16):
    drawn = deviation * jax.random.normal(own_key, shape, jnp.float32)
    if pieces:
        drawn = drawn * shard_levels(own_key, shape, pieces, -0.22, 0.18)
    return jnp.clip(drawn, -limit, limit).astype(kind)


def setup_inputs(seed: int = 0) -> dict:
    key_of = jax.random.split(jax.random.key(seed), 5)
    adjoint_rhs = centred(key_of[0], (N_LEAF, NRHS, DROWS), 1.0, 6.0, ((0, 8), (2, 4)), jnp.float32)
    panel_tiles = centred(key_of[1], (N_LEAF, SEP, PCOLS), (4 * SEP) ** -0.5, 0.0625, ((0, 8), (1, 4)))
    diag_inverse = centred(key_of[2], (N_LEAF, DROWS, SEP), SEP ** -0.5, 0.125, ((0, 8), (1, 4)))
    front_sizes = plant(jax.random.randint(key_of[3], (NODES,), SEP // 4, SEP + 1), jax.random.fold_in(key_of[3], 1), SEP // 4, SEP).astype(jnp.int32)
    return {"adjoint_rhs": adjoint_rhs, "panel_tiles": panel_tiles, "diag_inverse": diag_inverse, "front_sizes": front_sizes}


def ancestor_terms(pair):
    anc_blocks, tile_blocks = pair
    total = jnp.zeros((anc_blocks.shape[1], tile_blocks.shape[2]), jnp.float32)
    for upper in range(anc_blocks.shape[0]):
        total = total + jnp.dot(anc_blocks[upper], tile_blocks[upper], preferred_element_type=jnp.float32)
    return total


def apply_inverse(pair):
    return jnp.dot(pair[0], pair[1], preferred_element_type=jnp.float32)


def reference(adjoint_rhs, panel_tiles, diag_inverse, front_sizes):
    rows_per = DROWS // N_PANEL
    solved_low = []
    solved_full = []
    positions = jnp.arange(SEP)
    lower_mask = positions[None, :] <= positions[:, None]
    ident = (positions[None, :] == positions[:, None]).astype(jnp.float32)
    for height in range(LEVELS):
        group_size = N_LEAF >> height
        fronts = 1 << height
        col_width = SEP // group_size
        share = col_width // N_PANEL
        col_start = sum(upper * (SEP // (N_LEAF >> upper)) for upper in range(height))
        row_start = sum((SEP // (N_LEAF >> upper)) // N_PANEL for upper in range(height))
        right = adjoint_rhs.reshape(N_LEAF, NRHS, N_PANEL, rows_per)[:, :, :, row_start:row_start + share]
        right = right.reshape(fronts, group_size, NRHS, N_PANEL, share).transpose(0, 2, 1, 3, 4).reshape(fronts, NRHS, SEP)
        right = right.astype(jnp.float32)
        inverse_raw = diag_inverse.reshape(N_LEAF, N_PANEL, rows_per, SEP)[:, :, row_start:row_start + share, :]
        inverse_raw = inverse_raw.reshape(fronts, SEP, SEP).astype(jnp.float32)
        factor = (jnp.where(lower_mask[None], inverse_raw, 0.0) + ident[None]).astype(jnp.bfloat16)
        if height > 0:
            region = panel_tiles[:, :, col_start:col_start + height * col_width]
            region = region.reshape(fronts, group_size, SEP, height, col_width).transpose(0, 3, 2, 1, 4)
            region = region.reshape(fronts, height, SEP, SEP)
            ancestors = jnp.stack([jnp.repeat(solved_low[upper], 1 << (height - upper), axis=0) for upper in range(height)], axis=1)
            resid = right - lax.map(ancestor_terms, (ancestors, region))
        else:
            resid = right
        live_rows = front_sizes[fronts - 1:2 * fronts - 1]
        live = positions[None, None, :] < live_rows[:, None, None]
        resid_low = jnp.where(live, resid, 0.0).astype(jnp.bfloat16)
        solved = lax.map(apply_inverse, (resid_low, factor))
        solved_full.append(solved)
        solved_low.append(solved.astype(jnp.bfloat16))
    return jnp.stack([jnp.repeat(solved_full[height], N_LEAF >> height, axis=0) for height in range(LEVELS)], axis=1)
```

```python
import jax
import jax.numpy as jnp
from jax import lax
from jax.sharding import PartitionSpec as P


def swapped(block, axis, stride):
    count = lax.axis_size(axis)
    return lax.ppermute(block, axis, [(low, low ^ 1 << stride) for low in range(count)])


def halved(parts, axis_pos, axis, bit):
    mine = (axis_pos >> bit) & 1
    low, high = parts[: len(parts) // 2], parts[len(parts) // 2 :]
    keep = [jnp.where(mine == 0, a, b) for a, b in zip(low, high)]
    give = [jnp.where(mine == 0, b, a) for a, b in zip(low, high)]
    width = keep[0].shape[1]
    got = swapped(jnp.concatenate(give, axis=1), axis, bit)
    return [k + got[:, i * width : (i + 1) * width] for i, k in enumerate(keep)]


def scattered(partial_sum, axis_pos, axis):
    count = lax.axis_size(axis)
    bits = count.bit_length() - 1
    width = partial_sum.shape[1] // count
    blocks = [partial_sum[:, i * width : (i + 1) * width] for i in range(count)]
    order = sorted(range(count), key=lambda i: [(i >> b) & 1 for b in range(bits)])
    parts = [blocks[i] for i in order]
    for bit in range(bits):
        parts = halved(parts, axis_pos, axis, bit)
    return parts[0]


def per_device(adjoint_rhs, panel_tiles, diag_inverse, front_sizes):
    leaf_count = lax.axis_size("leaf")
    panel_count = lax.axis_size("panel")
    levels = leaf_count.bit_length()
    leaf_pos = lax.axis_index("leaf")
    panel_pos = lax.axis_index("panel")
    sep_rows = diag_inverse.shape[2]
    columns = jnp.arange(sep_rows)
    solved = []
    results = []
    for height in range(levels):
        group_size = leaf_count >> height
        col_width = sep_rows // group_size
        share = col_width // panel_count
        col_start = sum((upper * (sep_rows // (leaf_count >> upper)) for upper in range(height)))
        row_start = sum(
            (sep_rows // (leaf_count >> upper) // panel_count for upper in range(height))
        )
        front_pos = leaf_pos // group_size
        member = leaf_pos % group_size
        right = adjoint_rhs[0, :, row_start : row_start + share]
        if height > 0:
            partial_value = 0.0
            for upper in range(height):
                low = col_start + upper * col_width
                partial_value = partial_value + jnp.dot(
                    solved[upper],
                    panel_tiles[0, :, low : low + col_width],
                    preferred_element_type=jnp.float32,
                )
            resid = right - scattered(partial_value, panel_pos, "panel")
        else:
            resid = right
        front_id = (1 << height) - 1 + front_pos
        live_size = jnp.sum(jnp.where(jnp.arange(front_sizes.shape[0]) == front_id, front_sizes, 0))
        global_rows = member * col_width + panel_pos * share + jnp.arange(share)
        resid_low = jnp.where(global_rows[None, :] < live_size, resid, 0.0).astype(jnp.bfloat16)
        block = diag_inverse[0, row_start : row_start + share, :].astype(jnp.float32)
        below = columns[None, :] <= global_rows[:, None]
        factor = (
            jnp.where(below, block, 0.0)
            + (columns[None, :] == global_rows[:, None]).astype(jnp.float32)
        ).astype(jnp.bfloat16)
        terms = jnp.dot(resid_low, factor, preferred_element_type=jnp.float32)
        mine = scattered(terms, panel_pos, "panel")
        for bit in range(levels - 1 - height):
            mine = mine + swapped(mine, "leaf", bit)
        rows_now = mine.astype(jnp.bfloat16)
        solved.append(rows_now)
        results.append(mine)
    return jnp.stack(results, axis=0)[None]


def solution(mesh):
    in_specs = (P("leaf", None, "panel"), P("leaf", "panel", None), P("leaf", "panel", None), P())
    out_specs = P("leaf", None, None, "panel")
    return jax.shard_map(
        per_device, mesh=mesh, in_specs=in_specs, out_specs=out_specs, check_vma=False
    )
```

```python
import jax
import jax.numpy as jnp
from jax import lax
from jax.sharding import PartitionSpec as P


def exchanged(block, leaf_flip, panel_flip):
    leaf_count, panel_count = lax.axis_size("leaf"), lax.axis_size("panel")
    if leaf_flip == 0:
        return lax.ppermute(block, "panel", [(i, i ^ panel_flip) for i in range(panel_count)])
    if panel_flip == 0:
        return lax.ppermute(block, "leaf", [(i, i ^ leaf_flip) for i in range(leaf_count)])
    flip = leaf_flip * panel_count + panel_flip
    return lax.ppermute(
        block, ("leaf", "panel"), [(i, i ^ flip) for i in range(leaf_count * panel_count)]
    )


def chunk_order(count):
    bits = count.bit_length() - 1
    return sorted(range(count), key=lambda m: [-(m >> b & 1) for b in range(bits)])


def reduced(chunk_of, leaf_bits):
    count = lax.axis_size("panel")
    bits = count.bit_length() - 1
    held = {}
    arrived = {}
    for m in chunk_order(count):
        held[m] = chunk_of(m)
        if m & 1:
            arrived[m ^ 1] = exchanged(held[m], 0, 1)
    for bit in range(1, bits + 1):
        held = {m: held[m] + arrived[m] for m in arrived}
        arrived = {}
        if bit == bits:
            break
        step = 1 << bit
        if bit == bits - 1 and leaf_bits > 0:
            far, near = held[step], held[0]
            from_panel = exchanged(far, 0, step)
            from_leaf = exchanged(near, 1, 0)
            from_both = exchanged(far, 1, step)
            total = (near + from_panel) + (from_leaf + from_both)
            for leaf_bit in range(1, leaf_bits):
                total = total + exchanged(total, 1 << leaf_bit, 0)
            return total
        for m in sorted(held, reverse=True):
            if m & step:
                arrived[m ^ step] = exchanged(held[m], 0, step)
    return held[0]


def per_device(adjoint_rhs, panel_tiles, diag_inverse, front_sizes):
    leaf_count = lax.axis_size("leaf")
    panel_count = lax.axis_size("panel")
    levels = leaf_count.bit_length()
    leaf_pos = lax.axis_index("leaf")
    panel_pos = lax.axis_index("panel")
    sep_rows = diag_inverse.shape[2]
    strip = sep_rows // panel_count
    tiles = panel_tiles[0]
    inverse = diag_inverse[0]
    solved = []
    results = []
    base = {}

    def sizes(height):
        group_size = leaf_count >> height
        col_width = sep_rows // group_size
        share = col_width // panel_count
        col_start = sum((upper * (sep_rows // (leaf_count >> upper)) for upper in range(height)))
        row_start = sum(
            (sep_rows // (leaf_count >> upper) // panel_count for upper in range(height))
        )
        return group_size, col_width, share, col_start, row_start

    def own_rows(height):
        group_size, col_width, share, _, _ = sizes(height)
        return (leaf_pos % group_size) * col_width + panel_pos * share + jnp.arange(share)

    def masked(block, low, rows):
        columns = low + jnp.arange(block.shape[1])
        kept = jnp.where(columns[None, :] <= rows[:, None], block.astype(jnp.float32), 0.0)
        one = (columns[None, :] == rows[:, None]).astype(jnp.float32)
        return (kept + one).astype(jnp.bfloat16)

    def factor(height, m):
        _, _, share, _, row_start = sizes(height)
        low = (panel_pos ^ m) * strip
        block = lax.dynamic_slice(inverse, (row_start, low), (share, strip))
        return masked(block, low, own_rows(height))

    def coupling(height, m):
        _, col_width, share, col_start, _ = sizes(height)
        low = col_start + (height - 1) * col_width + (panel_pos ^ m) * share
        return lax.dynamic_slice(tiles, (0, low), (tiles.shape[0], share))

    def part(whole, m):
        width = whole.shape[1] // panel_count
        return lax.dynamic_slice(whole, (0, (panel_pos ^ m) * width), (whole.shape[0], width))

    factors = {}
    couplings = {}
    for height in range(1, levels):
        couplings[height] = lax.optimization_barrier(
            {m: coupling(height, m) for m in range(panel_count)}
        )
        factors[height] = lax.optimization_barrier(
            {m: factor(height, m) for m in range(panel_count)}
        )

    for height in range(levels):
        group_size, _, share, _, row_start = sizes(height)
        rows = own_rows(height)
        resid = adjoint_rhs[0, :, row_start : row_start + share]
        if height > 0:

            def update(m):
                term = jnp.dot(
                    solved[-1], couplings[height][m], preferred_element_type=jnp.float32
                )
                return term + part(base[height], m) if height in base else term

            resid = resid - reduced(update, 0)
        front_id = (1 << height) - 1 + leaf_pos // group_size
        live_size = lax.dynamic_slice(front_sizes, (front_id,), (1,)) if height else front_sizes[:1]
        resid_low = jnp.where(rows[None, :] < live_size[:, None], resid, 0.0).astype(jnp.bfloat16)
        if height == 0:
            whole = masked(inverse[row_start : row_start + share], 0, rows)
            terms = jnp.dot(resid_low, whole, preferred_element_type=jnp.float32)
            mine = reduced(lambda m: part(terms, m), levels - 1 - height)
        else:
            mine = reduced(
                lambda m: jnp.dot(
                    resid_low, factors[height][m], preferred_element_type=jnp.float32
                ),
                levels - 1 - height,
            )
        solved.append(mine.astype(jnp.bfloat16))
        results.append(mine)
        for later in range(height + 2, levels):
            _, width, _, start, _ = sizes(later)
            low = start + height * width
            term = jnp.dot(
                solved[-1], tiles[:, low : low + width], preferred_element_type=jnp.float32
            )
            base[later] = base[later] + term if later in base else term
    return jnp.stack(results, axis=0)[None]


def solution(mesh):
    in_specs = (P("leaf", None, "panel"), P("leaf", "panel", None), P("leaf", "panel", None), P())
    out_specs = P("leaf", None, None, "panel")

    return jax.shard_map(
        per_device, mesh=mesh, in_specs=in_specs, out_specs=out_specs, check_vma=False
    )
```

```python
import jax
import jax.numpy as jnp
from jax import lax
from jax.sharding import PartitionSpec as P


def exchanged(block, leaf_flip, panel_flip):
    leaf_count, panel_count = lax.axis_size("leaf"), lax.axis_size("panel")
    if leaf_flip == 0:
        return lax.ppermute(block, "panel", [(i, i ^ panel_flip) for i in range(panel_count)])
    if panel_flip == 0:
        return lax.ppermute(block, "leaf", [(i, i ^ leaf_flip) for i in range(leaf_count)])
    flip = leaf_flip * panel_count + panel_flip
    return lax.ppermute(
        block, ("leaf", "panel"), [(i, i ^ flip) for i in range(leaf_count * panel_count)]
    )


def chunk_order(count):
    bits = count.bit_length() - 1
    return sorted(range(count), key=lambda m: [-(m >> b & 1) for b in range(bits)])


def reduced(chunk_of, leaf_bits, direct=False, joined=False):
    count = lax.axis_size("panel")
    bits = count.bit_length() - 1
    held = {}
    arrived = {}
    if direct:
        total = None
        for m in range(count - 1, -1, -1):
            chunk = chunk_of(m)
            got = exchanged(chunk, 0, m) if m else chunk
            total = got if total is None else total + got
        return total
    for m in chunk_order(count):
        held[m] = chunk_of(m)
        if m & 1 and not joined:
            arrived[m ^ 1] = exchanged(held[m], 0, 1)
    if joined:
        odd = [m for m in held if m & 1]
        width = held[odd[0]].shape[1]
        got = exchanged(jnp.concatenate([held[m] for m in odd], axis=1), 0, 1)
        arrived = {m ^ 1: got[:, i * width : (i + 1) * width] for i, m in enumerate(odd)}
    for bit in range(1, bits + 1):
        held = {m: held[m] + arrived[m] for m in arrived}
        arrived = {}
        if bit == bits:
            break
        step = 1 << bit
        if bit == bits - 1 and leaf_bits > 0:
            far, near = held[step], held[0]
            from_panel = exchanged(far, 0, step)
            from_leaf = exchanged(near, 1, 0)
            from_both = exchanged(far, 1, step)
            total = (near + from_panel) + (from_leaf + from_both)
            for leaf_bit in range(1, leaf_bits):
                total = total + exchanged(total, 1 << leaf_bit, 0)
            return total
        for m in sorted(held, reverse=True):
            if m & step:
                arrived[m ^ step] = exchanged(held[m], 0, step)
    return held[0]


def exchanged_in_one(panel_count, share):
    return panel_count <= 4 and share <= 256


def per_device(adjoint_rhs, panel_tiles, diag_inverse, front_sizes):
    leaf_count = lax.axis_size("leaf")
    panel_count = lax.axis_size("panel")
    levels = leaf_count.bit_length()
    leaf_pos = lax.axis_index("leaf")
    panel_pos = lax.axis_index("panel")
    sep_rows = diag_inverse.shape[2]
    strip = sep_rows // panel_count
    tiles = panel_tiles[0]
    inverse = diag_inverse[0]
    solved = []
    results = []
    base = {}

    def sizes(height):
        group_size = leaf_count >> height
        col_width = sep_rows // group_size
        share = col_width // panel_count
        col_start = sum((upper * (sep_rows // (leaf_count >> upper)) for upper in range(height)))
        row_start = sum(
            (sep_rows // (leaf_count >> upper) // panel_count for upper in range(height))
        )
        return group_size, col_width, share, col_start, row_start

    def own_rows(height):
        group_size, col_width, share, _, _ = sizes(height)
        return (leaf_pos % group_size) * col_width + panel_pos * share + jnp.arange(share)

    def masked(block, low, rows):
        columns = low + jnp.arange(block.shape[1])
        kept = jnp.where(columns[None, :] <= rows[:, None], block.astype(jnp.float32), 0.0)
        one = (columns[None, :] == rows[:, None]).astype(jnp.float32)
        return (kept + one).astype(jnp.bfloat16)

    def factor(height, m):
        _, _, share, _, row_start = sizes(height)
        low = (panel_pos ^ m) * strip
        block = lax.dynamic_slice(inverse, (row_start, low), (share, strip))
        return masked(block, low, own_rows(height))

    def coupling(height, m):
        _, col_width, share, col_start, _ = sizes(height)
        low = col_start + (height - 1) * col_width + (panel_pos ^ m) * share
        return lax.dynamic_slice(tiles, (0, low), (tiles.shape[0], share))

    def part(whole, m):
        width = whole.shape[1] // panel_count
        return lax.dynamic_slice(whole, (0, (panel_pos ^ m) * width), (whole.shape[0], width))

    def alive(height):
        group_size, _, _, _, _ = sizes(height)
        front_id = (1 << height) - 1 + leaf_pos // group_size
        live_size = lax.dynamic_slice(front_sizes, (front_id,), (1,)) if height else front_sizes[:1]
        return (own_rows(height) < live_size)[None, :]

    def right_of(height):
        _, _, share, _, row_start = sizes(height)
        return adjoint_rhs[0, :, row_start : row_start + share]

    def in_one(height):
        return exchanged_in_one(panel_count, sizes(height)[2])

    factors = {}
    couplings = {}
    lives = {}
    rights = {}
    lives = lax.optimization_barrier({h: alive(h) for h in range(1, levels)})
    for height in range(1, levels):
        rights[height] = lax.optimization_barrier(right_of(height))
    for height in range(1, levels):
        couplings[height] = lax.optimization_barrier(
            {m: coupling(height, m) for m in range(panel_count)}
        )
        factors[height] = lax.optimization_barrier(
            {m: factor(height, m) for m in range(panel_count)}
        )

    for height in range(levels):
        _, _, share, _, row_start = sizes(height)
        rows = own_rows(height)
        if height == 0:
            resid = right_of(0)
            live = alive(0)
        else:
            live = lives[height]

            def update(m):
                term = jnp.dot(
                    solved[-1], couplings[height][m], preferred_element_type=jnp.float32
                )
                for early in base.get(height, ()):
                    term = term + part(early, m)
                return term

            resid = rights[height] - reduced(update, 0, direct=in_one(height))
        resid_low = jnp.where(live, resid, 0.0).astype(jnp.bfloat16)
        if height == 0:
            whole = masked(inverse[row_start : row_start + share], 0, rows)
            terms = jnp.dot(resid_low, whole, preferred_element_type=jnp.float32)
            mine = reduced(lambda m: part(terms, m), levels - 1 - height, joined=True)
        else:
            mine = reduced(
                lambda m: jnp.dot(
                    resid_low, factors[height][m], preferred_element_type=jnp.float32
                ),
                levels - 1 - height,
            )
        solved.append(mine.astype(jnp.bfloat16))
        results.append(mine)
        for later in range(height + 2, levels):
            _, width, _, start, _ = sizes(later)
            low = start + height * width
            term = jnp.dot(
                solved[-1], tiles[:, low : low + width], preferred_element_type=jnp.float32
            )
            base.setdefault(later, []).append(term)
    return jnp.stack(results, axis=0)[None]


def solution(mesh):
    in_specs = (P("leaf", None, "panel"), P("leaf", "panel", None), P("leaf", "panel", None), P())
    out_specs = P("leaf", None, None, "panel")

    return jax.shard_map(
        per_device, mesh=mesh, in_specs=in_specs, out_specs=out_specs, check_vma=False
    )
```

```python
import jax
import jax.numpy as jnp
from jax import lax
from jax.sharding import PartitionSpec as P


def exchanged(block, leaf_flip, panel_flip):
    leaf_count, panel_count = lax.axis_size("leaf"), lax.axis_size("panel")
    if leaf_flip == 0:
        return lax.ppermute(block, "panel", [(i, i ^ panel_flip) for i in range(panel_count)])
    if panel_flip == 0:
        return lax.ppermute(block, "leaf", [(i, i ^ leaf_flip) for i in range(leaf_count)])
    flip = leaf_flip * panel_count + panel_flip
    return lax.ppermute(
        block, ("leaf", "panel"), [(i, i ^ flip) for i in range(leaf_count * panel_count)]
    )


def chunk_order(count):
    bits = count.bit_length() - 1
    return sorted(range(count), key=lambda m: [-(m >> b & 1) for b in range(bits)])


def halves_reduced(far, near, leaf_bits, step):
    side = lax.axis_index("leaf") & 1
    rows = near.shape[0] // 2

    def half(block, flip):
        return lax.dynamic_slice(block, ((side ^ flip) * rows, 0), (rows, block.shape[1]))

    from_panel = exchanged(half(far, 0), 0, step)
    from_leaf = exchanged(half(near, 1), 1, 0)
    from_both = exchanged(half(far, 1), 1, step)
    total = (half(near, 0) + from_panel) + (from_leaf + from_both)
    for leaf_bit in range(leaf_bits - 1, 1, -1):
        total = total + exchanged(total, 1 << leaf_bit, 0)
    mine = total + exchanged(total, 2, 0)
    other = exchanged(total, 1, 0) + exchanged(total, 3, 0)
    low = jnp.where(side == 0, mine, other)
    high = jnp.where(side == 0, other, mine)
    return jnp.concatenate([low, high], axis=0)


def reduced(chunk_of, leaf_bits, direct=False, joined=False):
    count = lax.axis_size("panel")
    bits = count.bit_length() - 1
    held = {}
    arrived = {}
    if direct:
        total = None
        for m in direct_order(count):
            chunk = chunk_of(m)
            got = exchanged(chunk, 0, m) if m else chunk
            total = got if total is None else total + got
        return total
    for m in chunk_order(count):
        held[m] = chunk_of(m)
        if m & 1 and not joined:
            arrived[m ^ 1] = exchanged(held[m], 0, 1)
    if joined:
        odd = [m for m in held if m & 1]
        width = held[odd[0]].shape[1]
        got = exchanged(jnp.concatenate([held[m] for m in odd], axis=1), 0, 1)
        arrived = {m ^ 1: got[:, i * width : (i + 1) * width] for i, m in enumerate(odd)}
    for bit in range(1, bits + 1):
        held = {m: held[m] + arrived[m] for m in arrived}
        arrived = {}
        if bit == bits:
            break
        step = 1 << bit
        if bit == bits - 1 and leaf_bits > 0:
            far, near = held[step], held[0]
            if leaf_bits > 1:
                return halves_reduced(far, near, leaf_bits, step)
            from_panel = exchanged(far, 0, step)
            from_leaf = exchanged(near, 1, 0)
            from_both = exchanged(far, 1, step)
            return (near + from_panel) + (from_leaf + from_both)
        for m in sorted(held, reverse=True):
            if m & step:
                arrived[m ^ step] = exchanged(held[m], 0, step)
    return held[0]


def direct_order(count):
    half = count // 2
    return [m for m in range(half, count)] + [m for m in range(half - 1, -1, -1)]


def exchanged_in_one(panel_count, share):
    return panel_count <= 4 and share <= 256


def per_device(adjoint_rhs, panel_tiles, diag_inverse, front_sizes):
    leaf_count = lax.axis_size("leaf")
    panel_count = lax.axis_size("panel")
    levels = leaf_count.bit_length()
    leaf_pos = lax.axis_index("leaf")
    panel_pos = lax.axis_index("panel")
    sep_rows = diag_inverse.shape[2]
    strip = sep_rows // panel_count
    tiles = panel_tiles[0]
    inverse = diag_inverse[0]
    solved = []
    results = []
    base = {}

    def sizes(height):
        group_size = leaf_count >> height
        col_width = sep_rows // group_size
        share = col_width // panel_count
        col_start = sum((upper * (sep_rows // (leaf_count >> upper)) for upper in range(height)))
        row_start = sum(
            (sep_rows // (leaf_count >> upper) // panel_count for upper in range(height))
        )
        return group_size, col_width, share, col_start, row_start

    def own_rows(height):
        group_size, col_width, share, _, _ = sizes(height)
        return (leaf_pos % group_size) * col_width + panel_pos * share + jnp.arange(share)

    def masked(block, low, rows):
        columns = low + jnp.arange(block.shape[1])
        kept = jnp.where(columns[None, :] <= rows[:, None], block.astype(jnp.float32), 0.0)
        one = (columns[None, :] == rows[:, None]).astype(jnp.float32)
        return (kept + one).astype(jnp.bfloat16)

    def factor(height, m):
        _, _, share, _, row_start = sizes(height)
        low = (panel_pos ^ m) * strip
        block = lax.dynamic_slice(inverse, (row_start, low), (share, strip))
        return masked(block, low, own_rows(height))

    def coupling(height, m):
        _, col_width, share, col_start, _ = sizes(height)
        low = col_start + (height - 1) * col_width + (panel_pos ^ m) * share
        return lax.dynamic_slice(tiles, (0, low), (tiles.shape[0], share))

    def part(whole, m):
        width = whole.shape[1] // panel_count
        return lax.dynamic_slice(whole, (0, (panel_pos ^ m) * width), (whole.shape[0], width))

    def alive_later():
        total = sum(sizes(height)[2] for height in range(1, levels))
        place = jnp.arange(total)
        rows = live = jnp.zeros((total,), jnp.int32)
        start = 0
        for height in range(1, levels):
            group_size, col_width, share, _, _ = sizes(height)
            front_id = (1 << height) - 1 + leaf_pos // group_size
            first = (leaf_pos % group_size) * col_width + panel_pos * share
            here = place >= start
            rows = jnp.where(here, place - start + first, rows)
            live = jnp.where(here, lax.dynamic_slice(late_sizes, (front_id,), (1,)), live)
            start += share
        return (rows < live)[None, :]

    def right_of(height):
        _, _, share, _, row_start = sizes(height)
        return adjoint_rhs[0, :, row_start : row_start + share]

    def in_one(height):
        return exchanged_in_one(panel_count, sizes(height)[2])

    late_sizes = lax.optimization_barrier(front_sizes)
    factors = {}
    couplings = {}
    lives = {}
    rights = {}
    ends = lax.optimization_barrier(alive_later())
    start = 0
    for height in range(1, levels):
        share = sizes(height)[2]
        lives[height] = ends[:, start : start + share]
        start += share
    for height in range(1, levels):
        rights[height] = lax.optimization_barrier(right_of(height))
    for height in range(1, levels):
        couplings[height] = lax.optimization_barrier(
            {m: coupling(height, m) for m in range(panel_count)}
        )
        factors[height] = lax.optimization_barrier(
            {m: factor(height, m) for m in range(panel_count)}
        )

    for height in range(levels):
        _, _, share, _, row_start = sizes(height)
        rows = own_rows(height)
        if height == 0:
            resid = right_of(0)
            live = (own_rows(0) < front_sizes[:1])[None, :]
        else:
            live = lives[height]

            def update(m):
                term = jnp.dot(
                    solved[-1], couplings[height][m], preferred_element_type=jnp.float32
                )
                return term + part(base[height], m) if height in base else term

            resid = rights[height] - reduced(update, 0, direct=in_one(height))
        resid_low = jnp.where(live, resid, 0.0).astype(jnp.bfloat16)
        if height == 0:
            whole = masked(inverse[row_start : row_start + share], 0, rows)
            terms = jnp.dot(resid_low, whole, preferred_element_type=jnp.float32)
            mine = reduced(lambda m: part(terms, m), levels - 1 - height, joined=True)
        else:
            mine = reduced(
                lambda m: jnp.dot(
                    resid_low, factors[height][m], preferred_element_type=jnp.float32
                ),
                levels - 1 - height,
            )
        solved.append(mine.astype(jnp.bfloat16))
        results.append(mine)
        for later in range(height + 2, levels):
            _, width, _, start, _ = sizes(later)
            low = start + height * width
            term = jnp.dot(
                solved[-1], tiles[:, low : low + width], preferred_element_type=jnp.float32
            )
            base[later] = lax.optimization_barrier(base[later] + term if later in base else term)
    return jnp.stack(results, axis=0)[None]


def solution(mesh):
    in_specs = (P("leaf", None, "panel"), P("leaf", "panel", None), P("leaf", "panel", None), P())
    out_specs = P("leaf", None, None, "panel")

    return jax.shard_map(
        per_device, mesh=mesh, in_specs=in_specs, out_specs=out_specs, check_vma=False
    )
```

```python
import jax
import jax.numpy as jnp
from jax import lax
from jax.sharding import PartitionSpec as P


def exchanged(block, leaf_flip, panel_flip):
    leaf_count, panel_count = lax.axis_size("leaf"), lax.axis_size("panel")
    if leaf_flip == 0:
        return lax.ppermute(block, "panel", [(i, i ^ panel_flip) for i in range(panel_count)])
    if panel_flip == 0:
        return lax.ppermute(block, "leaf", [(i, i ^ leaf_flip) for i in range(leaf_count)])
    flip = leaf_flip * panel_count + panel_flip
    return lax.ppermute(
        block, ("leaf", "panel"), [(i, i ^ flip) for i in range(leaf_count * panel_count)]
    )


def chunk_order(count):
    bits = count.bit_length() - 1
    return sorted(range(count), key=lambda m: [-(m >> b & 1) for b in range(bits)])


def halves_reduced(far, near, leaf_bits, step):
    side = lax.axis_index("leaf") & 1
    rows = near.shape[0] // 2

    def half(block, flip):
        return lax.dynamic_slice(block, ((side ^ flip) * rows, 0), (rows, block.shape[1]))

    from_panel = exchanged(half(far, 0), 0, step)
    from_leaf = exchanged(half(near, 1), 1, 0)
    from_both = exchanged(half(far, 1), 1, step)
    total = (half(near, 0) + from_panel) + (from_leaf + from_both)
    for leaf_bit in range(leaf_bits - 1, 1, -1):
        total = total + exchanged(total, 1 << leaf_bit, 0)
    mine = total + exchanged(total, 2, 0)
    other = exchanged(total, 1, 0) + exchanged(total, 3, 0)
    low = jnp.where(side == 0, mine, other)
    high = jnp.where(side == 0, other, mine)
    return jnp.concatenate([low, high], axis=0)


def reduced(chunk_of, leaf_bits, direct=False, joined=False):
    count = lax.axis_size("panel")
    bits = count.bit_length() - 1
    held = {}
    arrived = {}
    if direct:
        total = None
        for m in direct_order(count):
            chunk = chunk_of(m)
            got = exchanged(chunk, 0, m) if m else lax.optimization_barrier(chunk)
            total = got if total is None else total + got
        return total
    for m in chunk_order(count):
        held[m] = chunk_of(m)
        if m & 1 and not joined:
            arrived[m ^ 1] = exchanged(held[m], 0, 1)
    if joined:
        odd = [m for m in held if m & 1]
        width = held[odd[0]].shape[1]
        got = exchanged(jnp.concatenate([held[m] for m in odd], axis=1), 0, 1)
        arrived = {m ^ 1: got[:, i * width : (i + 1) * width] for i, m in enumerate(odd)}
    for bit in range(1, bits + 1):
        held = {m: held[m] + arrived[m] for m in arrived}
        arrived = {}
        if bit == bits:
            break
        step = 1 << bit
        if bit == bits - 1 and leaf_bits > 0:
            far, near = held[step], held[0]
            if leaf_bits > 1:
                return halves_reduced(far, near, leaf_bits, step)
            from_panel = exchanged(far, 0, step)
            from_leaf = exchanged(near, 1, 0)
            from_both = exchanged(far, 1, step)
            return (near + from_panel) + (from_leaf + from_both)
        held[0] = lax.optimization_barrier(held[0])
        for m in sorted(held, reverse=True):
            if m & step:
                arrived[m ^ step] = exchanged(held[m], 0, step)
    return held[0]


def direct_order(count):
    return list(range(count - 1, -1, -1))


def exchanged_in_one(panel_count, share):
    return panel_count <= 4 and share <= 256


def per_device(adjoint_rhs, panel_tiles, diag_inverse, front_sizes):
    leaf_count = lax.axis_size("leaf")
    panel_count = lax.axis_size("panel")
    levels = leaf_count.bit_length()
    leaf_pos = lax.axis_index("leaf")
    panel_pos = lax.axis_index("panel")
    sep_rows = diag_inverse.shape[2]
    strip = sep_rows // panel_count
    tiles = panel_tiles[0]
    inverse = diag_inverse[0]
    solved = []
    results = []
    base = {}

    def sizes(height):
        group_size = leaf_count >> height
        col_width = sep_rows // group_size
        share = col_width // panel_count
        col_start = sum((upper * (sep_rows // (leaf_count >> upper)) for upper in range(height)))
        row_start = sum(
            (sep_rows // (leaf_count >> upper) // panel_count for upper in range(height))
        )
        return group_size, col_width, share, col_start, row_start

    def own_rows(height):
        group_size, col_width, share, _, _ = sizes(height)
        return (leaf_pos % group_size) * col_width + panel_pos * share + jnp.arange(share)

    def masked(block, low, rows):
        columns = low + jnp.arange(block.shape[1])
        kept = jnp.where(columns[None, :] <= rows[:, None], block.astype(jnp.float32), 0.0)
        one = (columns[None, :] == rows[:, None]).astype(jnp.float32)
        return (kept + one).astype(jnp.bfloat16)

    def factor(height, m):
        _, _, share, _, row_start = sizes(height)
        low = (panel_pos ^ m) * strip
        block = lax.dynamic_slice(inverse, (row_start, low), (share, strip))
        return masked(block, low, own_rows(height))

    def coupling(height, m):
        _, col_width, share, col_start, _ = sizes(height)
        low = col_start + (height - 1) * col_width + (panel_pos ^ m) * share
        return lax.dynamic_slice(tiles, (0, low), (tiles.shape[0], share))

    def part(whole, m):
        width = whole.shape[1] // panel_count
        return lax.dynamic_slice(whole, (0, (panel_pos ^ m) * width), (whole.shape[0], width))

    def alive_later():
        total = sum(sizes(height)[2] for height in range(1, levels))
        place = jnp.arange(total)
        rows = fronts = jnp.zeros((total,), jnp.int32)
        start = 0
        for height in range(1, levels):
            group_size, col_width, share, _, _ = sizes(height)
            front_id = (1 << height) - 1 + leaf_pos // group_size
            first = (leaf_pos % group_size) * col_width + panel_pos * share
            here = place >= start
            rows = jnp.where(here, place - start + first, rows)
            fronts = jnp.where(here, front_id, fronts)
            start += share
        chosen = jnp.arange(late_sizes.shape[0])[:, None] == fronts[None, :]
        live = jnp.sum(jnp.where(chosen, late_sizes[:, None], 0), axis=0)
        return (rows < live)[None, :]

    def right_of(height):
        _, _, share, _, row_start = sizes(height)
        return adjoint_rhs[0, :, row_start : row_start + share]

    def in_one(height):
        return exchanged_in_one(panel_count, sizes(height)[2])

    late_sizes = lax.optimization_barrier(front_sizes)
    factors = {}
    couplings = {}
    lives = {}
    rights = {}
    ends = lax.optimization_barrier(alive_later())
    start = 0
    for height in range(1, levels):
        share = sizes(height)[2]
        lives[height] = ends[:, start : start + share]
        start += share
    for height in range(1, levels):
        rights[height] = lax.optimization_barrier(right_of(height))
    for height in range(1, levels):
        couplings[height] = lax.optimization_barrier(
            {m: coupling(height, m) for m in range(panel_count)}
        )
        factors[height] = lax.optimization_barrier(
            {m: factor(height, m) for m in range(panel_count)}
        )

    for height in range(levels):
        _, _, share, _, row_start = sizes(height)
        rows = own_rows(height)
        if height == 0:
            resid = right_of(0)
            live = (own_rows(0) < front_sizes[:1])[None, :]
        else:
            live = lives[height]

            def update(m):
                term = jnp.dot(
                    solved[-1], couplings[height][m], preferred_element_type=jnp.float32
                )
                return term + part(base[height], m) if height in base else term

            resid = rights[height] - reduced(update, 0, direct=in_one(height))
        resid_low = jnp.where(live, resid, 0.0).astype(jnp.bfloat16)
        if height == 0:
            whole = masked(inverse[row_start : row_start + share], 0, rows)
            terms = jnp.dot(resid_low, whole, preferred_element_type=jnp.float32)
            mine = reduced(lambda m: part(terms, m), levels - 1 - height, joined=True)
        else:
            mine = reduced(
                lambda m: jnp.dot(
                    resid_low, factors[height][m], preferred_element_type=jnp.float32
                ),
                levels - 1 - height,
            )
        solved.append(mine.astype(jnp.bfloat16))
        results.append(mine)
        if height == levels - 2:
            early = jnp.stack(results + [jnp.zeros_like(mine)], axis=0)[None]
            early = lax.optimization_barrier(early)
        for later in range(height + 2, levels):
            _, width, _, start, _ = sizes(later)
            low = start + height * width
            term = jnp.dot(
                solved[-1], tiles[:, low : low + width], preferred_element_type=jnp.float32
            )
            base[later] = lax.optimization_barrier(base[later] + term if later in base else term)
    return lax.dynamic_update_slice(early, results[-1][None, None], (0, levels - 1, 0, 0))


def solution(mesh):
    in_specs = (P("leaf", None, "panel"), P("leaf", "panel", None), P("leaf", "panel", None), P())
    out_specs = P("leaf", None, None, "panel")

    return jax.shard_map(
        per_device, mesh=mesh, in_specs=in_specs, out_specs=out_specs, check_vma=False
    )
```
